128 devices in a mesh: row: 8 (over y, core), col: 16 (over z, x).
Axes of the slice: x: 4, y: 4, z: 4, core: 2. Of those that a mesh axis runs over, the one named last changes fastest.
Arguments:
- amplitudes: float32 [96, 256, 1024], P('col', None, 'row'), may hold values from -6 to 6
- interaction: float32 [16384, 16384], P('row', 'col'), may hold values from -0.5 to 0.5, as said below
- tile_counts: int32 [16], replicated, may hold values from 2 to 6, as said below
- tile_block: int32 [96], replicated, may hold values from -1 to 63, as said below
- recouple_sign: int32 [96], replicated, may hold values from 0 to 1
- orbit_perm: int32 [96, 256], replicated, may hold values from 0 to 255, each once within a row
- particle_energy: float32 [96, 256], P('col'), may hold values from -2 to 2
Outputs:
- sigma: float32 [96, 256, 1024], P('col', None, 'row')
The draws below stay inside these ranges and needn't reach their ends.
Inputs may be any that keep to these rules, and one draw needn't show every extreme that they name: Owner c holds its live tiles in its first tile_counts[c] slots; the counts sum to 64, and some owner holds 6. `tile_block`: live slots map one to one onto the 64 cross-channel tiles, and slots that are not live hold -1; two live tiles of one owner never lie in the same aligned group of 4 cross-channel tiles. interaction equals its transpose.
All inputs are finite; a program needn't handle non-finite values.
Results may differ from the reference program's by a relative error of at most 0.000061.
Values sent between devices are 32-bit elements; how exact they have to be, the bound alone decides.
A program may use at most 128 MiB of HBM per device.

```python
import jax
import jax.numpy as jnp
from jax import lax

TILE = 256
HCOLS = 1024
BLOCKS_DEV = 4
SLOTS = 6
BLOCKS = 64
ORDER = 16384
N_COL = 16


def shared_layout(key):
    folded = jax.random.fold_in(key, 11)
    key_pair, key_size, key_slot, key_target, key_within = jax.random.split(folded, 5)
    pairing = jax.random.permutation(key_pair, N_COL)
    spare_room = SLOTS - BLOCKS_DEV
    shifts = jax.random.randint(key_size, (N_COL // 2,), 0, spare_room + 1)
    shifts = shifts.at[0].set(spare_room)
    change = jnp.zeros((N_COL,), jnp.int32).at[pairing[0::2]].set(shifts).at[pairing[1::2]].set(-shifts)
    counts = (BLOCKS_DEV + change).astype(jnp.int32)
    starts = jnp.cumsum(counts) - counts
    slot_subkeys = jax.random.split(key_slot, N_COL)
    scramble = jax.vmap(lambda subkey: jax.random.permutation(subkey, SLOTS))(slot_subkeys)
    slot_ids = jnp.arange(SLOTS, dtype=jnp.int32)[None, :]
    is_live = slot_ids < counts[:, None]
    scores = jnp.where(is_live, scramble, SLOTS + slot_ids)
    ranking = jnp.argsort(jnp.argsort(scores, axis=1), axis=1)
    position = starts[:, None] + ranking
    relabel = jax.random.permutation(key_target, N_COL)
    target = relabel[position % N_COL]
    within_subkeys = jax.random.split(key_within, N_COL)
    within = jax.vmap(lambda subkey: jax.random.permutation(subkey, BLOCKS_DEV))(within_subkeys)
    blocks = target * BLOCKS_DEV + within[target, jnp.clip(position // N_COL, 0, BLOCKS_DEV - 1)]
    blocks = jnp.where(is_live, blocks, -1)
    return (counts, blocks.reshape(-1).astype(jnp.int32))


def draw_tile_counts(key, part):
    return shared_layout(key)[0]


def draw_tile_block(key, part):
    return shared_layout(key)[1]


def draw_interaction(key, part):
    key_main = jax.random.fold_in(jax.random.fold_in(key, 23), 0)
    normal_draw = jax.random.normal(key_main, (ORDER, ORDER), jnp.float32)
    symmetric = (normal_draw + normal_draw.T) * (0.5 / ORDER) ** 0.5
    return jnp.clip(symmetric, -0.5, 0.5)


def touch_ends(drawn, rng, low, high):
    longest = drawn.shape.index(max(drawn.shape))
    spots = []
    for shift in (0, 1):
        where = [jax.random.randint(jax.random.fold_in(rng, axis), (), 0, length) for axis, length in enumerate(drawn.shape)]
        where[longest] = (where[longest] + shift) % drawn.shape[longest]
        spots.append(tuple(where))
    return drawn.at[spots[0]].set(low).at[spots[1]].set(high)


def level_of(stream_key, shape, cuts, low, largest):
    factor_of, own = 1.0, jax.random.fold_in(stream_key, 6)
    for axis_at, blocks in cuts:
        heights = jnp.exp(jax.random.uniform(jax.random.fold_in(own, axis_at), (blocks,), jnp.float32, low / len(cuts), largest / len(cuts)))
        factor_of = factor_of * jnp.repeat(heights, shape[axis_at] // blocks).reshape([-1 if axis == axis_at else 1 for axis in range(len(shape))])
    return factor_of


def normal_values(own_key, extent, deviation, bound, pieces=(), kind=jnp.bfloat16):
    result = jax.random.normal(own_key, extent, jnp.float32) * deviation
    if len(pieces) > 0:
        result = level_of(own_key, extent, pieces, -0.22, 0.18) * result
    return jnp.clip(result, min=-bound, max=bound).astype(kind)


def setup_inputs(seed: int = 0) -> dict:
    splits = jax.random.split(jax.random.key(seed), 8)
    return {
        "amplitudes": normal_values(splits[0], (N_COL * SLOTS, TILE, HCOLS), 1.0, 6.0, ((0, 16), (2, 8)), jnp.float32),
        "interaction": draw_interaction(jax.random.fold_in(splits[7], 71), 0),
        "tile_counts": draw_tile_counts(jax.random.fold_in(splits[7], 71), 0),
        "tile_block": draw_tile_block(jax.random.fold_in(splits[7], 71), 0),
        "recouple_sign": touch_ends(jax.random.randint(splits[4], (N_COL * SLOTS,), 0, 2), jax.random.fold_in(splits[4], 1), 0, 1).astype(jnp.int32),
        "orbit_perm": jax.vmap(lambda own: jax.random.permutation(own, TILE))(jax.random.split(splits[5], (N_COL * SLOTS))).reshape((N_COL * SLOTS, TILE)).astype(jnp.int32),
        "particle_energy": jnp.clip(jax.random.uniform(splits[6], (N_COL * SLOTS, TILE), jnp.float32, -2.0, 2.0) * level_of(splits[6], (N_COL * SLOTS, TILE), ((0, 16),), -0.4, 0.0), -2.0, 2.0),
    }


def reorder_rows(tiles, orders):
    return jax.vmap(lambda single, ordering: jnp.take(single, ordering, axis=0))(tiles, orders)


def reference(amplitudes, interaction, tile_counts, tile_block, recouple_sign, orbit_perm, particle_energy):
    tile_total = amplitudes.shape[0]
    slot_ids = jnp.arange(tile_total, dtype=jnp.int32)
    owners = (slot_ids // SLOTS).astype(jnp.int32)
    is_live = (slot_ids % SLOTS) < jnp.take(tile_counts, owners)
    live_mask = is_live.astype(jnp.float32)[:, None, None]
    phases = (1 - 2 * recouple_sign).astype(jnp.float32)
    permuted = reorder_rows(amplitudes, orbit_perm) * phases[:, None, None]
    targets = jnp.where(is_live, tile_block, BLOCKS).astype(jnp.int32)
    cross_tiles = jnp.zeros((BLOCKS, TILE, HCOLS), jnp.float32).at[targets].set(permuted, mode="drop")
    image = jnp.dot(interaction, cross_tiles.reshape(ORDER, HCOLS), precision=lax.Precision.HIGHEST, preferred_element_type=jnp.float32)
    image = image.reshape(BLOCKS, TILE, HCOLS)
    picked = jnp.take(image, jnp.clip(tile_block, 0, BLOCKS - 1).astype(jnp.int32), axis=0)
    inverse = jnp.argsort(orbit_perm, axis=1).astype(jnp.int32)
    returned = reorder_rows(picked, inverse) * phases[:, None, None]
    sigma = (returned + particle_energy[:, :, None] * amplitudes) * live_mask
    return sigma
```

```python
import functools

import jax
import jax.numpy as jnp
from jax import lax
from jax.experimental import pallas as pl
from jax.experimental.pallas import tpu as pltpu
from jax.sharding import PartitionSpec as P

MESH = pl.DeviceIdType.MESH
F32, BF16 = jnp.float32, jnp.bfloat16
ROWS, COLS = 8, 16
SLOTS, TILE, LANES = 6, 256, 128
PIECE = TILE // COLS
STEPS = 4


def split3(v):
    a = v.astype(BF16)
    rest = v - a.astype(F32)
    b = rest.astype(BF16)
    d = (rest - b.astype(F32)).astype(BF16)
    return jnp.concatenate([a, b, d], axis=1)


def sum3(v):
    return v[:, :LANES] + v[:, LANES : 2 * LANES] + v[:, 2 * LANES :]


def kernel(
    counts, tblk, signs, tile_of, amp, perm, energy, w_hbm, out,
    onehot, send1, recv1, sel, xb, wst, whi, wlo, xhi, xlo, part, pin, rin,
    img, gb, ob, fin,
    wsem, s1, r1, s2, r2, sx, rx, sp, rp, sr, rr, s4, r4, s5, r5,
):
    row, col = lax.axis_index("row"), lax.axis_index("col")
    y, k = row // 2, row % 2
    z, x = col // 4, col % 4
    zp, zm, z2 = (z + 1) % 4, (z + 3) % 4, (z + 2) % 4
    xp, xm, x2 = (x + 1) % 4, (x + 3) % 4, (x + 2) % 4
    partner = row + 1 - 2 * k

    def rcopy(src, dst, ssem, rsem, to):
        return pltpu.make_async_remote_copy(
            src_ref=src, dst_ref=dst, send_sem=ssem, recv_sem=rsem,
            device_id=to, device_id_type=MESH,
        )

    barrier = pltpu.get_barrier_semaphore()

    @pl.loop(1, COLS)
    def _(d):
        pl.semaphore_signal(barrier, inc=1, device_id=(row, (col + d) % COLS), device_id_type=MESH)

    @pl.loop(1, ROWS)
    def _(d):
        pl.semaphore_signal(barrier, inc=1, device_id=((row + d) % ROWS, col), device_id_type=MESH)

    def wcopy(j):
        return pltpu.make_async_copy(w_hbm.at[:, j], wst.at[j], wsem.at[j])

    @pl.loop(0, COLS)
    def _(j):
        wcopy(j).start()

    row_iota = lax.broadcasted_iota(jnp.int32, (TILE, TILE), 0)
    col_iota = lax.broadcasted_iota(jnp.int32, (TILE, TILE), 1)

    @pl.loop(0, SLOTS)
    def _(s):
        order = perm[pl.ds(col * SLOTS + s, 1), :]
        phase = (1 - 2 * signs[col * SLOTS + s]).astype(F32)
        hot = jnp.where(row_iota == order, phase, 0.0)
        onehot[s] = hot.astype(BF16)
        moved = sum3(
            jnp.dot(hot.T.astype(BF16), split3(amp[s]), preferred_element_type=F32)
        )
        send1[:, pl.ds(s, 1)] = moved.reshape(COLS, 1, PIECE, LANES)

    pl.semaphore_wait(barrier, COLS - 1 + ROWS - 1)

    def spread_out(j):
        return rcopy(
            send1.at[j], recv1.at[pl.ds(col * SLOTS, SLOTS)], s1.at[j], r1.at[col], (row, j)
        )

    def spread_in(j):
        return rcopy(
            send1.at[j], recv1.at[pl.ds(j * SLOTS, SLOTS)], s1.at[j], r1.at[j], (row, j)
        )

    @pl.loop(1, COLS)
    def _(d):
        spread_out((col + d) % COLS).start()

    recv1[pl.ds(col * SLOTS, SLOTS)] = send1[col]

    @pl.loop(0, SLOTS)
    def _(s):
        diag = jnp.sum(
            jnp.where(row_iota == col_iota, energy[pl.ds(s, 1), :], 0.0), axis=1, keepdims=True
        )
        out[s] = diag * amp[s]

    @pl.loop(0, COLS // 2)
    def _(jp):
        wcopy(2 * jp).wait()
        wcopy(2 * jp + 1).wait()
        for mb in range(4):
            v = wst[pl.ds(2 * jp, 2), :, :, mb * TILE : (mb + 1) * TILE]
            v = v.reshape(TILE, TILE).T
            hi = v.astype(BF16)
            at = pl.ds(pl.multiple_of(jp * TILE, TILE), TILE)
            whi[mb * TILE : (mb + 1) * TILE, at] = hi
            wlo[mb * TILE : (mb + 1) * TILE, at] = (v - hi.astype(F32)).astype(BF16)

    @pl.loop(1, COLS)
    def _(d):
        spread_in((col + COLS - d) % COLS).wait_recv()

    @pl.loop(0, 64)
    def _(g):
        sel[g] = recv1[tile_of[g]]

    def rows_out(r):
        return rcopy(
            sel.at[pl.ds(r * 8, 8)], xb.at[row, z, x], s2.at[r], r2.at[row], (r, col)
        )

    def rows_in(r):
        return rcopy(sel.at[pl.ds(r * 8, 8)], xb.at[r, z, x], s2.at[r], r2.at[r], (r, col))

    @pl.loop(1, ROWS)
    def _(d):
        rows_out((row + d) % ROWS).start()

    xb[row, z, x] = sel[pl.ds(row * 8, 8)]

    @pl.loop(1, ROWS)
    def _(d):
        rows_in((row + d) % ROWS).wait_recv()

    def gather(s, kind, sends):
        h = 2 * ((y + 1 + s) % 4)
        g = h + 1
        refs = {
            (0, True): lambda: (xb.at[h, z, x], xb.at[h, z, x], xb.at[g, z, x], xb.at[g, z, x]),
            (0, False): lambda: (
                xb.at[h, z, xm], xb.at[h, z, xp], xb.at[g, zm, x], xb.at[g, zp, x]
            ),
            (1, True): lambda: (
                xb.at[h, z, xm, 0:4], xb.at[h, z, xp, 4:8],
                xb.at[g, zm, x, 0:4], xb.at[g, zp, x, 4:8],
            ),
            (1, False): lambda: (
                xb.at[h, z, x2, 0:4], xb.at[h, z, x2, 4:8],
                xb.at[g, z2, x, 0:4], xb.at[g, z2, x, 4:8],
            ),
            (2, True): lambda: (xb.at[h, z], xb.at[h, z], xb.at[g, :, x], xb.at[g, :, x]),
            (2, False): lambda: (xb.at[h, zm], xb.at[h, zp], xb.at[g, :, xm], xb.at[g, :, xp]),
            (3, True): lambda: (
                xb.at[h, zm, 0:2], xb.at[h, zp, 2:4], xb.at[g, 0:2, xm], xb.at[g, 2:4, xp]
            ),
            (3, False): lambda: (
                xb.at[h, z2, 0:2], xb.at[h, z2, 2:4], xb.at[g, 0:2, x2], xb.at[g, 2:4, x2]
            ),
        }[kind, sends]()
        along_x = ((row, z * 4 + xp), (row, z * 4 + xm))
        along_z = ((row, zp * 4 + x), (row, zm * 4 + x))
        to = along_x + along_z if kind < 2 else along_z + along_x
        return [
            rcopy(refs[n], refs[n], sx.at[s, kind, n], rx.at[s, kind, n], to[n])
            for n in range(4)
        ]

    def start(s, kind):
        for c in gather(s, kind, True):
            c.start()

    def arrived(s, kind):
        for c in gather(s, kind, False):
            c.wait_recv()

    @pl.loop(0, STEPS)
    def _(s):
        start(s, 0)

    @pl.loop(0, STEPS)
    def _(s):
        arrived(s, 0)
        start(s, 1)

    for s in range(2):
        arrived(s, 1)
        start(s, 2)
    arrived(0, 2)
    start(0, 3)

    def exchange(s):
        return rcopy(part.at[s, 1 - k], pin.at[s], sp.at[s], rp.at[s], (partner, col))

    def reduce_out(s):
        q = (y + 1 + s) % 4
        return rcopy(part.at[s, k], rin.at[s], sr.at[s], rr.at[s], (2 * q + k, col))

    def pair_sum(s):
        exchange(s).wait_recv()

        @pl.loop(0, 4)
        def _(m):
            at = pl.ds(m * TILE, TILE)
            part[s, k, at] = part[s, k, at] + pin[s, at]

        reduce_out(s).start()

    @pl.loop(0, STEPS)
    def _(s):
        @pl.when(s < STEPS - 2)
        def _():
            arrived(s + 2, 1)
            start(s + 2, 2)

        @pl.when(s < STEPS - 1)
        def _():
            arrived(s + 1, 2)
            start(s + 1, 3)

        @pl.when(s > 0)
        def _():
            pair_sum(s - 1)

        arrived(s, 3)
        h = 2 * ((y + 1 + s) % 4)

        @pl.loop(0, COLS // 2)
        def _(jp):
            at = (jp // 2, pl.ds(2 * (jp % 2), 2))
            va = xb[h, at[0], at[1]].reshape(TILE, LANES)
            vb = xb[h + 1, at[0], at[1]].reshape(TILE, LANES)
            v = jnp.concatenate([va, vb], axis=1)
            hi = v.astype(BF16)
            rows_at = pl.ds(pl.multiple_of(jp * TILE, TILE), TILE)
            xhi[rows_at, :] = hi
            xlo[rows_at, :] = (v - hi.astype(F32)).astype(BF16)

        @pl.loop(0, 4)
        def _(m):
            at = pl.ds(pl.multiple_of(m * TILE, TILE), TILE)
            acc = jnp.dot(whi[at, :], xlo[...], preferred_element_type=F32)
            acc += jnp.dot(wlo[at, :], xhi[...], preferred_element_type=F32)
            acc += jnp.dot(whi[at, :], xhi[...], preferred_element_type=F32)
            part[s, 0, at] = acc[:, :LANES]
            part[s, 1, at] = acc[:, LANES:]

        exchange(s).start()

    for s in range(STEPS - 1):
        reduce_out(s).wait_recv()
    exchange(STEPS - 1).wait_recv()

    @pl.loop(0, 4)
    def _(b):
        at = pl.ds(b * TILE, TILE)
        last = STEPS - 1
        v = part[last, k, at] + pin[last, at] + rin[0, at] + rin[1, at] + rin[2, at]
        img[:, pl.ds(b, 1)] = v.reshape(COLS, 1, PIECE, LANES)

    def back_out(j):
        return rcopy(img.at[j], gb.at[pl.ds(col * 4, 4)], s4.at[j], r4.at[col], (row, j))

    def back_in(j):
        return rcopy(img.at[j], gb.at[pl.ds(j * 4, 4)], s4.at[j], r4.at[j], (row, j))

    @pl.loop(1, COLS)
    def _(d):
        back_out((col + d) % COLS).start()

    gb[pl.ds(col * 4, 4)] = img[col]

    @pl.loop(1, COLS)
    def _(d):
        back_in((col + COLS - d) % COLS).wait_recv()

    @pl.loop(0, COLS * SLOTS)
    def _(i):
        ob[i] = gb[tblk[i]]

    def home_out(j):
        return rcopy(
            ob.at[pl.ds(j * SLOTS, SLOTS)], fin.at[col], s5.at[j], r5.at[col], (row, j)
        )

    def home_in(j):
        return rcopy(ob.at[pl.ds(j * SLOTS, SLOTS)], fin.at[j], s5.at[j], r5.at[j], (row, j))

    @pl.loop(1, COLS)
    def _(d):
        home_out((col + d) % COLS).start()

    fin[col] = ob[pl.ds(col * SLOTS, SLOTS)]

    @pl.loop(1, COLS)
    def _(d):
        home_in((col + COLS - d) % COLS).wait_recv()

    @pl.loop(0, SLOTS)
    def _(s):
        live = (s < counts[col]).astype(F32)
        v = fin[:, pl.ds(s, 1)].reshape(TILE, LANES)
        returned = sum3(jnp.dot(onehot[s], split3(v), preferred_element_type=F32))
        out[s] = (returned + out[s]) * live

    @pl.loop(1, COLS)
    def _(d):
        j = (col + d) % COLS
        spread_out(j).wait_send()
        back_out(j).wait_send()
        home_out(j).wait_send()

    @pl.loop(1, ROWS)
    def _(d):
        rows_out((row + d) % ROWS).wait_send()

    @pl.loop(0, STEPS)
    def _(s):
        for kind in range(4):
            for c in gather(s, kind, True):
                c.wait_send()
        exchange(s).wait_send()

    @pl.loop(0, STEPS - 1)
    def _(s):
        reduce_out(s).wait_send()


def local(
    amplitudes, interaction, tile_counts, tile_block, recouple_sign, orbit_perm, particle_energy
):
    tiles = jnp.arange(64, dtype=jnp.int32)
    slots = jnp.arange(COLS * SLOTS, dtype=jnp.int32)
    hit = tile_block[None, :] == tiles[:, None]
    tile_of = jnp.sum(jnp.where(hit, slots[None, :], 0), axis=1)
    tblk = jnp.clip(tile_block, 0, 63)
    w = interaction.reshape(8, COLS, PIECE, 1024)
    smem = pl.BlockSpec(memory_space=pltpu.SMEM)
    vmem = pl.BlockSpec(memory_space=pltpu.VMEM)
    dma = pltpu.SemaphoreType.DMA
    return pl.pallas_call(
        kernel,
        out_shape=jax.ShapeDtypeStruct(amplitudes.shape, F32),
        in_specs=[smem] * 4 + [vmem] * 3 + [pl.BlockSpec(memory_space=pl.ANY)],
        out_specs=vmem,
        scratch_shapes=[
            pltpu.VMEM((SLOTS, TILE, TILE), BF16),
            pltpu.VMEM((COLS, SLOTS, PIECE, LANES), F32),
            pltpu.VMEM((COLS * SLOTS, PIECE, LANES), F32),
            pltpu.VMEM((64, PIECE, LANES), F32),
            pltpu.VMEM((ROWS, 4, 4, 8, PIECE, LANES), F32),
            pltpu.VMEM((COLS, 8, PIECE, 1024), F32),
            pltpu.VMEM((1024, 2048), BF16),
            pltpu.VMEM((1024, 2048), BF16),
            pltpu.VMEM((2048, TILE), BF16),
            pltpu.VMEM((2048, TILE), BF16),
            pltpu.VMEM((STEPS, 2, 1024, LANES), F32),
            pltpu.VMEM((STEPS, 1024, LANES), F32),
            pltpu.VMEM((STEPS - 1, 1024, LANES), F32),
            pltpu.VMEM((COLS, 4, PIECE, LANES), F32),
            pltpu.VMEM((64, PIECE, LANES), F32),
            pltpu.VMEM((COLS * SLOTS, PIECE, LANES), F32),
            pltpu.VMEM((COLS, SLOTS, PIECE, LANES), F32),
            dma((COLS,)),
            dma((COLS,)), dma((COLS,)),
            dma((ROWS,)), dma((ROWS,)),
            dma((STEPS, 4, 4)), dma((STEPS, 4, 4)),
            dma((STEPS,)), dma((STEPS,)),
            dma((STEPS - 1,)), dma((STEPS - 1,)),
            dma((COLS,)), dma((COLS,)),
            dma((COLS,)), dma((COLS,)),
        ],
        compiler_params=pltpu.CompilerParams(
            collective_id=0, has_side_effects=True, vmem_limit_bytes=60 * 1024 * 1024
        ),
        name="sigma_step",
    )(tile_counts, tblk, recouple_sign, tile_of, amplitudes, orbit_perm, particle_energy, w)


def solution(mesh):
    placed = (P("col", None, "row"), P("row", "col"), P(), P(), P(), P(), P("col", None))
    return jax.shard_map(
        local, mesh=mesh, in_specs=placed, out_specs=P("col", None, "row"), check_vma=False
    )
```

```python
import functools

import jax
import jax.numpy as jnp
from jax import lax
from jax.experimental import pallas as pl
from jax.experimental.pallas import tpu as pltpu
from jax.sharding import PartitionSpec as P

MESH = pl.DeviceIdType.MESH
F32, BF16 = jnp.float32, jnp.bfloat16
ROWS, COLS = 8, 16
SLOTS, TILE, LANES = 6, 256, 128
PIECE = TILE // COLS
STEPS = 4
HALF = 512


def split3(v):
    a = v.astype(BF16)
    rest = v - a.astype(F32)
    b = rest.astype(BF16)
    d = (rest - b.astype(F32)).astype(BF16)
    return jnp.concatenate([a, b, d], axis=1)


def sum3(v):
    return v[:, :LANES] + v[:, LANES : 2 * LANES] + v[:, 2 * LANES :]


def kernel(
    counts, tblk, signs, tile_of, amp, perm, energy, w_hbm, out,
    onehot, send1, recv1, sel, xb, wst, whi, wlo, xhi, xlo, part, pin, relay, rin,
    img, gb0, gb1, ob, fin,
    wsem, s1, r1, s2, r2, sx, rx, sp, rp, sy, ry, sr, rr, s4, r4, s5, r5,
):
    row, col = lax.axis_index("row"), lax.axis_index("col")
    y, k = row // 2, row % 2
    z, x = col // 4, col % 4
    zp, zm, z2 = (z + 1) % 4, (z + 3) % 4, (z + 2) % 4
    xp, xm, x2 = (x + 1) % 4, (x + 3) % 4, (x + 2) % 4
    yp, ym, y2 = (y + 1) % 4, (y + 3) % 4, (y + 2) % 4
    partner = row + 1 - 2 * k
    last = STEPS - 1
    held = (gb0, gb1)

    def rcopy(src, dst, ssem, rsem, to):
        return pltpu.make_async_remote_copy(
            src_ref=src, dst_ref=dst, send_sem=ssem, recv_sem=rsem,
            device_id=to, device_id_type=MESH,
        )

    barrier = pltpu.get_barrier_semaphore()

    @pl.loop(1, COLS)
    def _(d):
        pl.semaphore_signal(barrier, inc=1, device_id=(row, (col + d) % COLS), device_id_type=MESH)

    @pl.loop(1, ROWS)
    def _(d):
        pl.semaphore_signal(barrier, inc=1, device_id=((row + d) % ROWS, col), device_id_type=MESH)

    def wcopy(j):
        return pltpu.make_async_copy(w_hbm.at[:, j], wst.at[j], wsem.at[j])

    @pl.loop(0, COLS)
    def _(j):
        wcopy(j).start()

    row_iota = lax.broadcasted_iota(jnp.int32, (TILE, TILE), 0)
    col_iota = lax.broadcasted_iota(jnp.int32, (TILE, TILE), 1)

    @pl.loop(0, SLOTS)
    def _(s):
        order = perm[pl.ds(col * SLOTS + s, 1), :]
        phase = (1 - 2 * signs[col * SLOTS + s]).astype(F32)
        hot = jnp.where(row_iota == order, phase, 0.0)
        onehot[s] = hot.astype(BF16)
        moved = sum3(
            jnp.dot(hot.T.astype(BF16), split3(amp[s]), preferred_element_type=F32)
        )
        send1[:, pl.ds(s, 1)] = moved.reshape(COLS, 1, PIECE, LANES)

    pl.semaphore_wait(barrier, COLS - 1 + ROWS - 1)

    def spread(j, slot):
        return rcopy(
            send1.at[j], recv1.at[pl.ds(slot * SLOTS, SLOTS)], s1.at[j], r1.at[slot], (row, j)
        )

    @pl.loop(1, COLS)
    def _(d):
        spread((col + d) % COLS, col).start()

    recv1[pl.ds(col * SLOTS, SLOTS)] = send1[col]

    @pl.loop(0, COLS // 2)
    def _(jp):
        wcopy(2 * jp).wait()
        wcopy(2 * jp + 1).wait()
        at = pl.ds(pl.multiple_of(jp * TILE, TILE), TILE)
        for b in range(4):
            v = wst[pl.ds(2 * jp, 2), :, :, b * TILE : (b + 1) * TILE]
            v = v.reshape(TILE, TILE).T
            hi = v.astype(BF16)
            lo = (v - hi.astype(F32)).astype(BF16)
            for m in range(2):
                rows_at = slice(m * HALF + b * LANES, m * HALF + (b + 1) * LANES)
                whi[rows_at, at] = hi[m * LANES : (m + 1) * LANES]
                wlo[rows_at, at] = lo[m * LANES : (m + 1) * LANES]

    @pl.loop(1, COLS)
    def _(d):
        j = (col + COLS - d) % COLS
        spread(j, j).wait_recv()

    @pl.loop(0, 64, unroll=8)
    def _(g):
        sel[g] = recv1[tile_of[g]]

    def rows_copy(r, slot):
        return rcopy(
            sel.at[pl.ds(r * 8, 8)], xb.at[slot, z, x], s2.at[r], r2.at[slot], (r, col)
        )

    for r in (2 * y2, 2 * y2 + 1, 2 * yp, 2 * ym, 2 * yp + 1, 2 * ym + 1, partner):
        rows_copy(r, row).start()

    xb[row, z, x] = sel[pl.ds(row * 8, 8)]

    def rows_arrived(*rs):
        for r in rs:
            rows_copy(r, r).wait_recv()

    chunk = (
        (2 * y2, 2 * y2 + 1), (2 * yp, 2 * ym), (2 * yp + 1, 2 * ym + 1), (2 * y, 2 * y + 1),
    )
    to_x = ((row, z * 4 + xp), (row, z * 4 + xm))
    to_z = ((row, zp * 4 + x), (row, zm * 4 + x))

    def gather(s, kind, sends):
        h, g = chunk[s]
        lo, up = slice(0, 2), slice(2, 4)
        refs = {
            (0, True): lambda: (xb.at[h, z, x], xb.at[h, z, x], xb.at[g, z, x], xb.at[g, z, x]),
            (0, False): lambda: (
                xb.at[h, z, xm], xb.at[h, z, xp], xb.at[g, zm, x], xb.at[g, zp, x]
            ),
            (1, True): lambda: (
                xb.at[h, z, xm, 0:4], xb.at[h, z, xp, 4:8],
                xb.at[g, zm, x, 0:4], xb.at[g, zp, x, 4:8],
            ),
            (1, False): lambda: (
                xb.at[h, z, x2, 0:4], xb.at[h, z, x2, 4:8],
                xb.at[g, z2, x, 0:4], xb.at[g, z2, x, 4:8],
            ),
            (2, True): lambda: (
                xb.at[h, z, lo], xb.at[h, z, up], xb.at[g, lo, x], xb.at[g, up, x]
            ),
            (2, False): lambda: (
                xb.at[h, zm, lo], xb.at[h, zp, up], xb.at[g, lo, xm], xb.at[g, up, xp]
            ),
            (3, True): lambda: (
                xb.at[h, z, up], xb.at[h, z, lo], xb.at[g, up, x], xb.at[g, lo, x]
            ),
            (3, False): lambda: (
                xb.at[h, zm, up], xb.at[h, zp, lo], xb.at[g, up, xm], xb.at[g, lo, xp]
            ),
            (4, True): lambda: (
                xb.at[h, zm, lo], xb.at[h, zp, up], xb.at[g, lo, xm], xb.at[g, up, xp]
            ),
            (4, False): lambda: (
                xb.at[h, z2, lo], xb.at[h, z2, up], xb.at[g, lo, x2], xb.at[g, up, x2]
            ),
        }[kind, sends]()
        to = to_x + to_z if kind < 2 else to_z + to_x
        return [
            rcopy(refs[n], refs[n], sx.at[s, kind, n], rx.at[s, kind, n], to[n])
            for n in range(4)
        ]

    def start(s, *kinds):
        for kind in kinds:
            for c in gather(s, kind, True):
                c.start()

    def arrived(s, *kinds):
        for kind in kinds:
            for c in gather(s, kind, False):
                c.wait_recv()

    def exchange(s, m):
        return rcopy(
            part.at[s, 1 - k, m], pin.at[s, m], sp.at[s, m], rp.at[s, m], (partner, col)
        )

    def relay_copy(m, slot, to):
        return rcopy(part.at[0, k, m], relay.at[slot], sy.at[m], ry.at[slot], to)

    def relay_out(m):
        return relay_copy(m, k, (2 * yp, col) if m == 0 else (2 * ym + 1, col))

    def relay_in(slot):
        return relay_copy(0, slot, (partner, col))

    def reduce_out(s, m):
        q = yp + k * (ym - yp)
        return rcopy(
            part.at[s, k, m], rin.at[k, m], sr.at[s - 1, m], rr.at[k, m], (2 * q + s - 1, col)
        )

    def reduce_in(n, m):
        return rcopy(part.at[1, k, m], rin.at[n, m], sr.at[0, m], rr.at[n, m], (partner, col))

    def dots(s, m):
        @pl.loop(0, 2)
        def _(n):
            at = pl.ds(pl.multiple_of(m * HALF + n * TILE, TILE), TILE)
            to = pl.ds(pl.multiple_of(n * TILE, TILE), TILE)
            acc = jnp.dot(whi[at, :], xlo[...], preferred_element_type=F32)
            acc += jnp.dot(wlo[at, :], xhi[...], preferred_element_type=F32)
            acc += jnp.dot(whi[at, :], xhi[...], preferred_element_type=F32)
            part[s, 0, m, to] = acc[:, :LANES]
            part[s, 1, m, to] = acc[:, LANES:]

        exchange(s, m).start()

    def convert(s):
        h, g = chunk[s]

        @pl.loop(0, COLS // 2)
        def _(jp):
            pair = pl.ds(2 * (jp % 2), 2)
            va = xb[h, jp // 2, pair].reshape(TILE, LANES)
            vb = xb[g, jp // 2, pair].reshape(TILE, LANES)
            v = jnp.concatenate([va, vb], axis=1)
            hi = v.astype(BF16)
            at = pl.ds(pl.multiple_of(jp * TILE, TILE), TILE)
            xhi[at, :] = hi
            xlo[at, :] = (v - hi.astype(F32)).astype(BF16)

    def back(m, j, slot):
        return rcopy(
            img.at[m, j], held[m].at[pl.ds(slot * 4, 4)], s4.at[m, j], r4.at[m, slot], (row, j)
        )

    def home(m, j, slot):
        return rcopy(
            ob.at[m, pl.ds(j * SLOTS, SLOTS)], fin.at[m, slot], s5.at[m, j], r5.at[m, slot],
            (row, j),
        )

    def finish(m):
        exchange(last, m).wait_recv()
        reduce_in(0, m).wait_recv()
        reduce_in(1, m).wait_recv()
        v = part[last, k, m] + pin[last, m] + rin[0, m] + rin[1, m]
        v = v.reshape(4, COLS, 1, 8, LANES)
        for b in range(4):
            img[m, :, b : b + 1] = v[b]

        @pl.loop(1, COLS)
        def _(d):
            back(m, (col + d) % COLS, col).start()

        held[m][pl.ds(col * 4, 4)] = img[m, col]

    def send_home(m):
        @pl.loop(1, COLS)
        def _(d):
            j = (col + COLS - d) % COLS
            back(m, j, j).wait_recv()

        @pl.loop(0, COLS * SLOTS, unroll=8)
        def _(i):
            ob[m, i] = held[m][jnp.maximum(tblk[i], 0)]

        @pl.loop(1, COLS)
        def _(d):
            home(m, (col + d) % COLS, col).start()

        fin[m, col] = ob[m, pl.ds(col * SLOTS, SLOTS)]

    rows_arrived(partner)
    start(3, 0)
    rows_arrived(2 * y2, 2 * y2 + 1)
    start(0, 0)
    rows_arrived(2 * yp, 2 * ym)
    start(1, 0)
    arrived(3, 0)
    start(3, 1)
    arrived(0, 0)
    start(0, 1)
    rows_arrived(2 * yp + 1, 2 * ym + 1)
    start(2, 0)
    arrived(0, 1)
    start(0, 2, 3)
    arrived(1, 0)
    start(1, 1)
    arrived(2, 0)
    start(2, 1)
    arrived(1, 1)
    start(1, 2, 3)
    arrived(0, 2)
    start(0, 4)

    for s in range(STEPS):
        if s + 2 < STEPS:
            arrived(s + 2, 1)
            start(s + 2, 2, 3)
        if s + 1 < STEPS:
            arrived(s + 1, 2)
            start(s + 1, 4)
        arrived(s, 3, 4)
        convert(s)
        if s == last:
            for m in range(2):
                dots(s, m)
                finish(m)
            break
        dots(s, 0)
        dots(s, 1)
        for m in range(2):
            exchange(s, m).wait_recv()
            part[s, k, m] = part[s, k, m] + pin[s, m]
            if s == 0:
                relay_out(m).start()
        if s > 0:
            relay_in(s - 1).wait_recv()
            part[s, k, k] = part[s, k, k] + relay[s - 1]
            for m in range(2):
                reduce_out(s, m).start()

    send_home(0)
    send_home(1)

    @pl.loop(0, SLOTS)
    def _(s):
        diag = jnp.sum(
            jnp.where(row_iota == col_iota, energy[pl.ds(s, 1), :], 0.0), axis=1, keepdims=True
        )
        out[s] = diag * amp[s]

    for m in range(2):
        @pl.loop(1, COLS)
        def _(d):
            j = (col + COLS - d) % COLS
            home(m, j, j).wait_recv()

    @pl.loop(0, SLOTS)
    def _(s):
        live = (s < counts[col]).astype(F32)
        v = fin[:, :, pl.ds(s, 1)].reshape(TILE, LANES)
        returned = sum3(jnp.dot(onehot[s], split3(v), preferred_element_type=F32))
        out[s] = (returned + out[s]) * live

    @pl.loop(1, COLS)
    def _(d):
        j = (col + d) % COLS
        spread(j, col).wait_send()
        for m in range(2):
            back(m, j, col).wait_send()
            home(m, j, col).wait_send()

    @pl.loop(1, ROWS)
    def _(d):
        rows_copy((row + d) % ROWS, row).wait_send()

    for s in range(STEPS):
        for kind in range(5):
            for c in gather(s, kind, True):
                c.wait_send()
        for m in range(2):
            exchange(s, m).wait_send()
    for m in range(2):
        relay_out(m).wait_send()
        for s in (1, 2):
            reduce_out(s, m).wait_send()


def local(
    amplitudes, interaction, tile_counts, tile_block, recouple_sign, orbit_perm, particle_energy
):
    tiles = jnp.arange(64, dtype=jnp.int32)
    slots = jnp.arange(COLS * SLOTS, dtype=jnp.int32)
    hit = tile_block[None, :] == tiles[:, None]
    tile_of = jnp.sum(jnp.where(hit, slots[None, :], 0), axis=1)
    w = interaction.reshape(8, COLS, PIECE, 1024)
    smem = pl.BlockSpec(memory_space=pltpu.SMEM)
    vmem = pl.BlockSpec(memory_space=pltpu.VMEM)
    dma = pltpu.SemaphoreType.DMA
    return pl.pallas_call(
        kernel,
        out_shape=jax.ShapeDtypeStruct(amplitudes.shape, F32),
        in_specs=[smem] * 4 + [vmem] * 3 + [pl.BlockSpec(memory_space=pl.ANY)],
        out_specs=vmem,
        scratch_shapes=[
            pltpu.VMEM((SLOTS, TILE, TILE), BF16),
            pltpu.VMEM((COLS, SLOTS, PIECE, LANES), F32),
            pltpu.VMEM((COLS * SLOTS, PIECE, LANES), F32),
            pltpu.VMEM((64, PIECE, LANES), F32),
            pltpu.VMEM((ROWS, 4, 4, 8, PIECE, LANES), F32),
            pltpu.VMEM((COLS, 8, PIECE, 1024), F32),
            pltpu.VMEM((1024, 2048), BF16),
            pltpu.VMEM((1024, 2048), BF16),
            pltpu.VMEM((2048, TILE), BF16),
            pltpu.VMEM((2048, TILE), BF16),
            pltpu.VMEM((STEPS, 2, 2, HALF, LANES), F32),
            pltpu.VMEM((STEPS, 2, HALF, LANES), F32),
            pltpu.VMEM((2, HALF, LANES), F32),
            pltpu.VMEM((2, 2, HALF, LANES), F32),
            pltpu.VMEM((2, COLS, 4, 8, LANES), F32),
            pltpu.VMEM((64, 8, LANES), F32),
            pltpu.VMEM((64, 8, LANES), F32),
            pltpu.VMEM((2, COLS * SLOTS, 8, LANES), F32),
            pltpu.VMEM((2, COLS, SLOTS, 8, LANES), F32),
            dma((COLS,)),
            dma((COLS,)), dma((COLS,)),
            dma((ROWS,)), dma((ROWS,)),
            dma((STEPS, 5, 4)), dma((STEPS, 5, 4)),
            dma((STEPS, 2)), dma((STEPS, 2)),
            dma((2,)), dma((2,)),
            dma((2, 2)), dma((2, 2)),
            dma((2, COLS)), dma((2, COLS)),
            dma((2, COLS)), dma((2, COLS)),
        ],
        compiler_params=pltpu.CompilerParams(
            collective_id=0, has_side_effects=True, vmem_limit_bytes=60 * 1024 * 1024
        ),
        name="sigma_step",
    )(tile_counts, tile_block, recouple_sign, tile_of, amplitudes, orbit_perm, particle_energy, w)


def solution(mesh):
    placed = (P("col", None, "row"), P("row", "col"), P(), P(), P(), P(), P("col", None))
    return jax.shard_map(
        local, mesh=mesh, in_specs=placed, out_specs=P("col", None, "row"), check_vma=False
    )
```

```python
import functools

import jax
import jax.numpy as jnp
from jax import lax
from jax.experimental import pallas as pl
from jax.experimental.pallas import tpu as pltpu
from jax.sharding import PartitionSpec as P

MESH = pl.DeviceIdType.MESH
F32, BF16 = jnp.float32, jnp.bfloat16
ROWS, COLS = 8, 16
SLOTS, TILE, LANES = 6, 256, 128
PIECE = TILE // COLS
STEPS = 4
HALF = 512


def split3(v):
    a = v.astype(BF16)
    rest = v - a.astype(F32)
    b = rest.astype(BF16)
    d = (rest - b.astype(F32)).astype(BF16)
    return jnp.concatenate([a, b, d], axis=1)


def sum3(v):
    return v[:, :LANES] + v[:, LANES : 2 * LANES] + v[:, 2 * LANES :]


def kernel(
    counts, tblk, signs, tile_of, amp, perm, energy, w_hbm, out,
    onehot, send1, recv1, sel, xa, xc, wst, whi, wlo, xhi, xlo, part, pin, relay, rin,
    img, gb0, gb1, ob, fin,
    wsem, s1, r1, s2, r2, sx, rx, sp, rp, sy, ry, sr, rr, s4, r4, s5, r5,
):
    row, col = lax.axis_index("row"), lax.axis_index("col")
    y, k = row // 2, row % 2
    z, x = col // 4, col % 4
    zp, zm, z2 = (z + 1) % 4, (z + 3) % 4, (z + 2) % 4
    xp, xm, x2 = (x + 1) % 4, (x + 3) % 4, (x + 2) % 4
    yp, ym, y2 = (y + 1) % 4, (y + 3) % 4, (y + 2) % 4
    partner = row + 1 - 2 * k
    last = STEPS - 1
    held = (gb0, gb1)

    def rcopy(src, dst, ssem, rsem, to):
        return pltpu.make_async_remote_copy(
            src_ref=src, dst_ref=dst, send_sem=ssem, recv_sem=rsem,
            device_id=to, device_id_type=MESH,
        )

    barrier = pltpu.get_barrier_semaphore()

    @pl.loop(1, COLS)
    def _(d):
        pl.semaphore_signal(barrier, inc=1, device_id=(row, (col + d) % COLS), device_id_type=MESH)

    @pl.loop(1, ROWS)
    def _(d):
        pl.semaphore_signal(barrier, inc=1, device_id=((row + d) % ROWS, col), device_id_type=MESH)

    def wcopy(j):
        return pltpu.make_async_copy(w_hbm.at[:, j], wst.at[j // 4, j % 4], wsem.at[j])

    @pl.loop(0, COLS)
    def _(j):
        wcopy(j).start()

    row_iota = lax.broadcasted_iota(jnp.int32, (TILE, TILE), 0)
    col_iota = lax.broadcasted_iota(jnp.int32, (TILE, TILE), 1)

    @pl.loop(0, SLOTS)
    def _(s):
        order = perm[pl.ds(col * SLOTS + s, 1), :]
        phase = (1 - 2 * signs[col * SLOTS + s]).astype(F32)
        hot = jnp.where(row_iota == order, phase, 0.0)
        onehot[s] = hot.astype(BF16)
        moved = sum3(
            jnp.dot(hot.T.astype(BF16), split3(amp[s]), preferred_element_type=F32)
        )
        send1[:, pl.ds(s, 1)] = moved.reshape(COLS, 1, PIECE, LANES)

    pl.semaphore_wait(barrier, COLS - 1 + ROWS - 1)

    def spread(j, slot):
        return rcopy(
            send1.at[j], recv1.at[pl.ds(slot * SLOTS, SLOTS)], s1.at[j], r1.at[slot], (row, j)
        )

    @pl.loop(1, COLS)
    def _(d):
        spread((col + d) % COLS, col).start()

    recv1[pl.ds(col * SLOTS, SLOTS)] = send1[col]

    @pl.loop(0, COLS)
    def _(j):
        wcopy(j).wait()

    def shift_of(n):
        return n + n // 2 - 2 * (n // 3)

    def place_a(n):
        return pl.ds(pl.multiple_of((n + 3 * (n // 3)) * TILE, TILE), TILE)

    def place_c(n):
        return pl.ds(pl.multiple_of((n + 3 + n // 3) * TILE, TILE), TILE)

    def weights(v, b, at):
        v = v.reshape(TILE, TILE).T
        hi = v.astype(BF16)
        lo = (v - hi.astype(F32)).astype(BF16)
        for m in range(2):
            rows_at = slice(m * HALF + b * LANES, m * HALF + (b + 1) * LANES)
            whi[rows_at, at] = hi[m * LANES : (m + 1) * LANES]
            wlo[rows_at, at] = lo[m * LANES : (m + 1) * LANES]

    @pl.loop(0, 4)
    def _(n):
        zn, xn = (z + shift_of(n)) % 4, (x + shift_of(n)) % 4
        for b in range(4):
            cut = slice(b * TILE, (b + 1) * TILE)
            weights(wst[zn, :, 0:4, :, cut], b, place_a(n))
            weights(wst[:, xn, 4:8, :, cut], b, place_c(n))

    @pl.loop(1, COLS)
    def _(d):
        j = (col + COLS - d) % COLS
        spread(j, j).wait_recv()

    @pl.loop(0, 64, unroll=8)
    def _(g):
        sel[g] = recv1[tile_of[g]]

    def rows_copies(r, source, slot):
        return [
            rcopy(
                sel.at[pl.ds(r * 8, 4)], xa.at[slot[0], z, x, slot[1]],
                s2.at[r, 0], r2.at[source, 0], (r, col),
            ),
            rcopy(
                sel.at[pl.ds(r * 8 + 4, 4)], xc.at[slot[0], x, z, slot[1]],
                s2.at[r, 1], r2.at[source, 1], (r, col),
            ),
        ]

    rows_sent = [
        c
        for r, slot in (
            (2 * y2, (0, k)), (2 * y2 + 1, (0, k)),
            (2 * ym, (1 + k, 0)), (2 * yp, (1 + k, 1)),
            (2 * ym + 1, (1 + k, 0)), (2 * yp + 1, (1 + k, 1)),
            (partner, (3, k)),
        )
        for c in rows_copies(r, row, slot)
    ]
    for c in rows_sent:
        c.start()

    xa[3, z, x, k] = sel[pl.ds(row * 8, 4)]
    xc[3, x, z, k] = sel[pl.ds(row * 8 + 4, 4)]

    def rows_arrived(s):
        for r, slot in (
            ((2 * y2, (0, 0)), (2 * y2 + 1, (0, 1))),
            ((2 * yp, (1, 0)), (2 * ym, (1, 1))),
            ((2 * yp + 1, (2, 0)), (2 * ym + 1, (2, 1))),
            ((partner, (3, 1 - k)),),
        )[s]:
            for c in rows_copies(r, r, slot):
                c.wait_recv()

    to_x = ((row, z * 4 + xp), (row, z * 4 + xm))
    to_z = ((row, zp * 4 + x), (row, zm * 4 + x))

    def gather(s, kind, sends):
        lo, up = slice(0, 2), slice(2, 4)
        if kind == 0:
            here, there = ((z, x), (z, x), (x, z), (x, z)), ((z, xm), (z, xp), (x, zm), (x, zp))
        elif kind == 1:
            here = ((z, xm, 0), (z, xp, 1), (x, zm, 0), (x, zp, 1))
            there = ((z, x2, 0), (z, x2, 1), (x, z2, 0), (x, z2, 1))
        elif kind == 2:
            here = ((z, lo), (z, up), (x, lo), (x, up))
            there = ((zm, lo), (zp, up), (xm, lo), (xp, up))
        elif kind == 3:
            here = ((z, up), (z, lo), (x, up), (x, lo))
            there = ((zm, up), (zp, lo), (xm, up), (xp, lo))
        else:
            here = ((zm, lo), (zp, up), (xm, lo), (xp, up))
            there = ((z2, lo), (z2, up), (x2, lo), (x2, up))
        to = to_x + to_z if kind < 2 else to_z + to_x
        copies = []
        for n, at in enumerate(here if sends else there):
            ref = (xa, xa, xc, xc)[n].at[(s,) + at]
            copies.append(rcopy(ref, ref, sx.at[s, kind, n], rx.at[s, kind, n], to[n]))
        return copies

    def start(s, *kinds):
        for kind in kinds:
            for c in gather(s, kind, True):
                c.start()

    def arrived(s, *kinds):
        for kind in kinds:
            for c in gather(s, kind, False):
                c.wait_recv()

    def exchange(s, m):
        return rcopy(
            part.at[s, 1 - k, m], pin.at[s, m], sp.at[s, m], rp.at[s, m], (partner, col)
        )

    def relay_copy(m, slot, to):
        return rcopy(part.at[0, k, m], relay.at[slot], sy.at[m], ry.at[slot], to)

    def relay_out(m):
        return relay_copy(m, k, (2 * yp, col) if m == 0 else (2 * ym + 1, col))

    def relay_in(slot):
        return relay_copy(0, slot, (partner, col))

    def reduce_out(s, m):
        q = yp + k * (ym - yp)
        return rcopy(
            part.at[s, k, m], rin.at[k, m], sr.at[s - 1, m], rr.at[k, m], (2 * q + s - 1, col)
        )

    def reduce_in(n, m):
        return rcopy(part.at[1, k, m], rin.at[n, m], sr.at[0, m], rr.at[n, m], (partner, col))

    def dots(s, m, first):
        rows_at = slice(m * HALF, (m + 1) * HALF)
        cut = slice(0, 6 * TILE) if first else slice(6 * TILE, 8 * TILE)
        hi = whi[rows_at, cut]
        both = jnp.concatenate([hi, wlo[rows_at, cut]], axis=0)
        both = jnp.dot(both, xhi[cut], preferred_element_type=F32)
        acc = jnp.dot(hi, xlo[cut], preferred_element_type=F32)
        acc += both[HALF:] + both[:HALF]
        for n in range(2):
            v = acc[:, n * LANES : (n + 1) * LANES]
            part[s, n, m] = v if first else part[s, n, m] + v

    def convert(v0, v1, at):
        v = jnp.concatenate([v0.reshape(TILE, LANES), v1.reshape(TILE, LANES)], axis=1)
        hi = v.astype(BF16)
        xhi[at, :] = hi
        xlo[at, :] = (v - hi.astype(F32)).astype(BF16)

    def convert_lines(s, low, high):
        @pl.loop(low, high)
        def _(n):
            zn, xn = (z + shift_of(n)) % 4, (x + shift_of(n)) % 4
            convert(xa[s, zn, :, 0], xa[s, zn, :, 1], place_a(n))
            convert(xc[s, xn, :, 0], xc[s, xn, :, 1], place_c(n))

    def near_part(s):
        convert_lines(s, 0, 3)
        dots(s, 0, True)
        dots(s, 1, True)

    def far_part(s):
        convert_lines(s, 3, 4)
        for m in range(2):
            dots(s, m, False)
            exchange(s, m).start()

    def row_sums(s):
        for m in range(2):
            exchange(s, m).wait_recv()
            part[s, k, m] = part[s, k, m] + pin[s, m]
            if s == 0:
                relay_out(m).start()
        if s > 0:
            relay_in(s - 1).wait_recv()
            part[s, k, k] = part[s, k, k] + relay[s - 1]
            for m in range(2):
                reduce_out(s, m).start()

    def back(m, j, slot):
        return rcopy(
            img.at[m, j], held[m].at[pl.ds(slot * 4, 4)], s4.at[m, j], r4.at[m, slot], (row, j)
        )

    def home(m, j, slot):
        return rcopy(
            ob.at[m, pl.ds(j * SLOTS, SLOTS)], fin.at[m, slot], s5.at[m, j], r5.at[m, slot],
            (row, j),
        )

    def finish(m):
        exchange(last, m).wait_recv()
        reduce_in(0, m).wait_recv()
        reduce_in(1, m).wait_recv()
        v = part[last, k, m] + pin[last, m] + rin[0, m] + rin[1, m]
        v = v.reshape(4, COLS, 1, 8, LANES)
        for b in range(4):
            img[m, :, b : b + 1] = v[b]

        @pl.loop(1, COLS)
        def _(d):
            back(m, (col + d) % COLS, col).start()

        held[m][pl.ds(col * 4, 4)] = img[m, col]

    def send_home(m):
        @pl.loop(1, COLS)
        def _(d):
            j = (col + COLS - d) % COLS
            back(m, j, j).wait_recv()

        @pl.loop(0, COLS * SLOTS, unroll=8)
        def _(i):
            ob[m, i] = held[m][jnp.maximum(tblk[i], 0)]

        @pl.loop(1, COLS)
        def _(d):
            home(m, (col + d) % COLS, col).start()

        fin[m, col] = ob[m, pl.ds(col * SLOTS, SLOTS)]

    rows_arrived(3)
    start(3, 0)
    rows_arrived(0)
    start(0, 0)
    rows_arrived(1)
    start(1, 0)
    arrived(3, 0)
    start(3, 1)
    rows_arrived(2)
    start(2, 0)
    for s in range(3):
        arrived(s, 0)
        start(s, 1)
    arrived(0, 1)
    start(0, 2, 3)
    arrived(1, 1)
    start(1, 2, 3)
    arrived(0, 2)
    start(0, 4)
    arrived(2, 1)
    start(2, 2, 3)
    arrived(0, 3)
    near_part(0)
    arrived(1, 2)
    start(1, 4)
    arrived(1, 3)
    near_part(1)
    arrived(0, 4)
    far_part(0)
    row_sums(0)
    arrived(2, 2)
    start(2, 4)
    arrived(3, 1)
    start(3, 2, 3)
    arrived(2, 3)
    near_part(2)
    arrived(1, 4)
    far_part(1)
    row_sums(1)
    arrived(2, 4)
    far_part(2)
    row_sums(2)
    arrived(3, 2)
    start(3, 4)
    arrived(3, 3)
    near_part(3)
    arrived(3, 4)
    far_part(3)
    finish(0)
    finish(1)
    send_home(0)
    send_home(1)

    @pl.loop(0, SLOTS)
    def _(s):
        diag = jnp.sum(
            jnp.where(row_iota == col_iota, energy[pl.ds(s, 1), :], 0.0), axis=1, keepdims=True
        )
        out[s] = diag * amp[s]

    for m in range(2):
        @pl.loop(1, COLS)
        def _(d):
            j = (col + COLS - d) % COLS
            home(m, j, j).wait_recv()

    @pl.loop(0, SLOTS)
    def _(s):
        live = (s < counts[col]).astype(F32)
        v = fin[:, :, pl.ds(s, 1)].reshape(TILE, LANES)
        returned = sum3(jnp.dot(onehot[s], split3(v), preferred_element_type=F32))
        out[s] = (returned + out[s]) * live

    @pl.loop(1, COLS)
    def _(d):
        j = (col + d) % COLS
        spread(j, col).wait_send()
        for m in range(2):
            back(m, j, col).wait_send()
            home(m, j, col).wait_send()

    for c in rows_sent:
        c.wait_send()

    for s in range(STEPS):
        for kind in range(5):
            for c in gather(s, kind, True):
                c.wait_send()
        for m in range(2):
            exchange(s, m).wait_send()
    for m in range(2):
        relay_out(m).wait_send()
        for s in (1, 2):
            reduce_out(s, m).wait_send()


def local(
    amplitudes, interaction, tile_counts, tile_block, recouple_sign, orbit_perm, particle_energy
):
    tiles = jnp.arange(64, dtype=jnp.int32)
    slots = jnp.arange(COLS * SLOTS, dtype=jnp.int32)
    hit = tile_block[None, :] == tiles[:, None]
    tile_of = jnp.sum(jnp.where(hit, slots[None, :], 0), axis=1)
    w = interaction.reshape(8, COLS, PIECE, 1024)
    smem = pl.BlockSpec(memory_space=pltpu.SMEM)
    vmem = pl.BlockSpec(memory_space=pltpu.VMEM)
    dma = pltpu.SemaphoreType.DMA
    return pl.pallas_call(
        kernel,
        out_shape=jax.ShapeDtypeStruct(amplitudes.shape, F32),
        in_specs=[smem] * 4 + [vmem] * 3 + [pl.BlockSpec(memory_space=pl.ANY)],
        out_specs=vmem,
        scratch_shapes=[
            pltpu.VMEM((SLOTS, TILE, TILE), BF16),
            pltpu.VMEM((COLS, SLOTS, PIECE, LANES), F32),
            pltpu.VMEM((COLS * SLOTS, PIECE, LANES), F32),
            pltpu.VMEM((64, PIECE, LANES), F32),
            pltpu.VMEM((STEPS, 4, 4, 2, 4, PIECE, LANES), F32),
            pltpu.VMEM((STEPS, 4, 4, 2, 4, PIECE, LANES), F32),
            pltpu.VMEM((4, 4, 8, PIECE, 1024), F32),
            pltpu.VMEM((1024, 2048), BF16),
            pltpu.VMEM((1024, 2048), BF16),
            pltpu.VMEM((2048, TILE), BF16),
            pltpu.VMEM((2048, TILE), BF16),
            pltpu.VMEM((STEPS, 2, 2, HALF, LANES), F32),
            pltpu.VMEM((STEPS, 2, HALF, LANES), F32),
            pltpu.VMEM((2, HALF, LANES), F32),
            pltpu.VMEM((2, 2, HALF, LANES), F32),
            pltpu.VMEM((2, COLS, 4, 8, LANES), F32),
            pltpu.VMEM((64, 8, LANES), F32),
            pltpu.VMEM((64, 8, LANES), F32),
            pltpu.VMEM((2, COLS * SLOTS, 8, LANES), F32),
            pltpu.VMEM((2, COLS, SLOTS, 8, LANES), F32),
            dma((COLS,)),
            dma((COLS,)), dma((COLS,)),
            dma((ROWS, 2)), dma((ROWS, 2)),
            dma((STEPS, 5, 4)), dma((STEPS, 5, 4)),
            dma((STEPS, 2)), dma((STEPS, 2)),
            dma((2,)), dma((2,)),
            dma((2, 2)), dma((2, 2)),
            dma((2, COLS)), dma((2, COLS)),
            dma((2, COLS)), dma((2, COLS)),
        ],
        compiler_params=pltpu.CompilerParams(
            collective_id=0, has_side_effects=True, vmem_limit_bytes=60 * 1024 * 1024
        ),
        name="sigma_step",
    )(tile_counts, tile_block, recouple_sign, tile_of, amplitudes, orbit_perm, particle_energy, w)


def solution(mesh):
    placed = (P("col", None, "row"), P("row", "col"), P(), P(), P(), P(), P("col", None))
    return jax.shard_map(
        local, mesh=mesh, in_specs=placed, out_specs=P("col", None, "row"), check_vma=False
    )
```

```python
import functools

import jax
import jax.numpy as jnp
from jax import lax
from jax.experimental import pallas as pl
from jax.experimental.pallas import tpu as pltpu
from jax.sharding import PartitionSpec as P

MESH = pl.DeviceIdType.MESH
F32, BF16 = jnp.float32, jnp.bfloat16
ROWS, COLS = 8, 16
SLOTS, TILE, LANES = 6, 256, 128
PIECE = TILE // COLS
STEPS = 4
HALF = 512


def split3(v):
    a = v.astype(BF16)
    rest = v - a.astype(F32)
    b = rest.astype(BF16)
    d = (rest - b.astype(F32)).astype(BF16)
    return jnp.concatenate([a, b, d], axis=1)


def sum3(v):
    return v[:, :LANES] + v[:, LANES : 2 * LANES] + v[:, 2 * LANES :]


def kernel(
    counts, tblk, signs, amp, perm, energy, w_hbm, out, slot_row, slot_of,
    onehot, send1, recv1, sel, xa, xc, wst, whi, wlo, xhi, xlo, part, pin, relay, rin,
    img, gb0, gb1, ob, fin,
    isem, wsem, s1, r1, s2, r2, sx, rx, sp, rp, sy, ry, sr, rr, s4, r4, s5, r5,
):
    row, col = lax.axis_index("row"), lax.axis_index("col")
    y, k = row // 2, row % 2
    z, x = col // 4, col % 4
    zp, zm, z2 = (z + 1) % 4, (z + 3) % 4, (z + 2) % 4
    xp, xm, x2 = (x + 1) % 4, (x + 3) % 4, (x + 2) % 4
    yp, ym, y2 = (y + 1) % 4, (y + 3) % 4, (y + 2) % 4
    partner = row + 1 - 2 * k
    last = STEPS - 1
    held = (gb0, gb1)

    def rcopy(src, dst, ssem, rsem, to):
        return pltpu.make_async_remote_copy(
            src_ref=src, dst_ref=dst, send_sem=ssem, recv_sem=rsem,
            device_id=to, device_id_type=MESH,
        )

    barrier = pltpu.get_barrier_semaphore()

    @pl.loop(1, COLS)
    def _(d):
        pl.semaphore_signal(barrier, inc=1, device_id=(row, (col + d) % COLS), device_id_type=MESH)

    @pl.loop(1, ROWS)
    def _(d):
        pl.semaphore_signal(barrier, inc=1, device_id=((row + d) % ROWS, col), device_id_type=MESH)

    def wcopy(j):
        return pltpu.make_async_copy(w_hbm.at[:, j], wst.at[j // 4, j % 4], wsem.at[j])

    @pl.loop(0, COLS)
    def _(j):
        wcopy(j).start()

    lane = lax.broadcasted_iota(jnp.int32, (8, LANES), 1)
    found = jnp.zeros((8, LANES), jnp.int32)
    for i in range(COLS * SLOTS):
        found = jnp.where(lane == tblk[i], i, found)
    slot_row[...] = found
    to_scalars = pltpu.make_async_copy(slot_row, slot_of, isem)
    to_scalars.start()

    row_iota = lax.broadcasted_iota(jnp.int32, (TILE, TILE), 0)
    col_iota = lax.broadcasted_iota(jnp.int32, (TILE, TILE), 1)

    @pl.loop(0, SLOTS)
    def _(s):
        order = perm[pl.ds(col * SLOTS + s, 1), :]
        phase = (1 - 2 * signs[col * SLOTS + s]).astype(F32)
        hot = jnp.where(row_iota == order, phase, 0.0)
        onehot[s] = hot.astype(BF16)
        moved = sum3(
            jnp.dot(hot.T.astype(BF16), split3(amp[s]), preferred_element_type=F32)
        )
        send1[:, pl.ds(s, 1)] = moved.reshape(COLS, 1, PIECE, LANES)

    pl.semaphore_wait(barrier, COLS - 1 + ROWS - 1)

    def spread(j, slot):
        return rcopy(
            send1.at[j], recv1.at[pl.ds(slot * SLOTS, SLOTS)], s1.at[j], r1.at[slot], (row, j)
        )

    @pl.loop(1, COLS)
    def _(d):
        spread((col + d) % COLS, col).start()

    recv1[pl.ds(col * SLOTS, SLOTS)] = send1[col]

    @pl.loop(0, COLS)
    def _(j):
        wcopy(j).wait()

    def shift_of(n):
        return n + n // 2 - 2 * (n // 3)

    def place_a(n):
        return pl.ds(pl.multiple_of((n + 3 * (n // 3)) * TILE, TILE), TILE)

    def place_c(n):
        return pl.ds(pl.multiple_of((n + 3 + n // 3) * TILE, TILE), TILE)

    def weights(v, b, at):
        v = v.reshape(TILE, TILE).T
        hi = v.astype(BF16)
        lo = (v - hi.astype(F32)).astype(BF16)
        for m in range(2):
            rows_at = slice(m * HALF + b * LANES, m * HALF + (b + 1) * LANES)
            whi[rows_at, at] = hi[m * LANES : (m + 1) * LANES]
            wlo[rows_at, at] = lo[m * LANES : (m + 1) * LANES]

    @pl.loop(0, 4)
    def _(n):
        zn, xn = (z + shift_of(n)) % 4, (x + shift_of(n)) % 4
        for b in range(4):
            cut = slice(b * TILE, (b + 1) * TILE)
            weights(wst[zn, :, 0:4, :, cut], b, place_a(n))
            weights(wst[:, xn, 4:8, :, cut], b, place_c(n))

    @pl.loop(1, COLS)
    def _(d):
        j = (col + COLS - d) % COLS
        spread(j, j).wait_recv()

    to_scalars.wait()

    @pl.loop(0, 64, unroll=32)
    def _(g):
        sel[g] = recv1[slot_of[0, g]]

    def rows_copies(r, source, slot):
        return [
            rcopy(
                sel.at[pl.ds(r * 8, 4)], xa.at[slot[0], z, x, slot[1]],
                s2.at[r, 0], r2.at[source, 0], (r, col),
            ),
            rcopy(
                sel.at[pl.ds(r * 8 + 4, 4)], xc.at[slot[0], x, z, slot[1]],
                s2.at[r, 1], r2.at[source, 1], (r, col),
            ),
        ]

    rows_sent = [
        c
        for r, slot in (
            (2 * y2, (0, k)), (2 * y2 + 1, (0, k)),
            (2 * ym, (1 + k, 0)), (2 * yp, (1 + k, 1)),
            (2 * ym + 1, (1 + k, 0)), (2 * yp + 1, (1 + k, 1)),
            (partner, (3, k)),
        )
        for c in rows_copies(r, row, slot)
    ]
    for c in rows_sent:
        c.start()

    xa[3, z, x, k] = sel[pl.ds(row * 8, 4)]
    xc[3, x, z, k] = sel[pl.ds(row * 8 + 4, 4)]

    def rows_arrived(s):
        for r, slot in (
            ((2 * y2, (0, 0)), (2 * y2 + 1, (0, 1))),
            ((2 * yp, (1, 0)), (2 * ym, (1, 1))),
            ((2 * yp + 1, (2, 0)), (2 * ym + 1, (2, 1))),
            ((partner, (3, 1 - k)),),
        )[s]:
            for c in rows_copies(r, r, slot):
                c.wait_recv()

    to_x = ((row, z * 4 + xp), (row, z * 4 + xm))
    to_z = ((row, zp * 4 + x), (row, zm * 4 + x))

    def gather(s, kind, sends):
        lo, up = slice(0, 2), slice(2, 4)
        if kind == 0:
            here, there = ((z, x), (z, x), (x, z), (x, z)), ((z, xm), (z, xp), (x, zm), (x, zp))
        elif kind == 1:
            here = ((z, xm, 0), (z, xp, 1), (x, zm, 0), (x, zp, 1))
            there = ((z, x2, 0), (z, x2, 1), (x, z2, 0), (x, z2, 1))
        elif kind == 2:
            here = ((z, lo), (z, up), (x, lo), (x, up))
            there = ((zm, lo), (zp, up), (xm, lo), (xp, up))
        elif kind == 3:
            here = ((z, up), (z, lo), (x, up), (x, lo))
            there = ((zm, up), (zp, lo), (xm, up), (xp, lo))
        else:
            here = ((zm, lo), (zp, up), (xm, lo), (xp, up))
            there = ((z2, lo), (z2, up), (x2, lo), (x2, up))
        to = to_x + to_z if kind < 2 else to_z + to_x
        copies = []
        for n, at in enumerate(here if sends else there):
            ref = (xa, xa, xc, xc)[n].at[(s,) + at]
            copies.append(rcopy(ref, ref, sx.at[s, kind, n], rx.at[s, kind, n], to[n]))
        return copies

    def start(s, *kinds):
        for kind in kinds:
            for c in gather(s, kind, True):
                c.start()

    def arrived(s, *kinds):
        for kind in kinds:
            for c in gather(s, kind, False):
                c.wait_recv()

    def exchange(s, m):
        return rcopy(
            part.at[s, 1 - k, m], pin.at[s, m], sp.at[s, m], rp.at[s, m], (partner, col)
        )

    def relay_copy(m, slot, to):
        return rcopy(part.at[0, k, m], relay.at[slot], sy.at[m], ry.at[slot], to)

    def relay_out(m):
        return relay_copy(m, k, (2 * yp, col) if m == 0 else (2 * ym + 1, col))

    def relay_in(slot):
        return relay_copy(0, slot, (partner, col))

    def reduce_out(s, m):
        q = yp + k * (ym - yp)
        return rcopy(
            part.at[s, k, m], rin.at[k, m], sr.at[s - 1, m], rr.at[k, m], (2 * q + s - 1, col)
        )

    def reduce_in(n, m):
        return rcopy(part.at[1, k, m], rin.at[n, m], sr.at[0, m], rr.at[n, m], (partner, col))

    def dots(s, m, first):
        rows_at = slice(m * HALF, (m + 1) * HALF)
        cut = slice(0, 6 * TILE) if first else slice(6 * TILE, 8 * TILE)
        hi = whi[rows_at, cut]
        both = jnp.concatenate([hi, wlo[rows_at, cut]], axis=0)
        both = jnp.dot(both, xhi[cut], preferred_element_type=F32)
        acc = jnp.dot(hi, xlo[cut], preferred_element_type=F32)
        acc += both[HALF:] + both[:HALF]
        for n in range(2):
            v = acc[:, n * LANES : (n + 1) * LANES]
            part[s, n, m] = v if first else part[s, n, m] + v

    def convert(v0, v1, at):
        v = jnp.concatenate([v0.reshape(TILE, LANES), v1.reshape(TILE, LANES)], axis=1)
        hi = v.astype(BF16)
        xhi[at, :] = hi
        xlo[at, :] = (v - hi.astype(F32)).astype(BF16)

    def convert_lines(s, low, high):
        @pl.loop(low, high)
        def _(n):
            zn, xn = (z + shift_of(n)) % 4, (x + shift_of(n)) % 4
            convert(xa[s, zn, :, 0], xa[s, zn, :, 1], place_a(n))
            convert(xc[s, xn, :, 0], xc[s, xn, :, 1], place_c(n))

    def near_part(s):
        convert_lines(s, 0, 3)
        dots(s, 0, True)
        dots(s, 1, True)

    def far_part(s):
        convert_lines(s, 3, 4)
        for m in range(2):
            dots(s, m, False)
            exchange(s, m).start()

    def row_sums(s):
        for m in range(2):
            exchange(s, m).wait_recv()
            part[s, k, m] = part[s, k, m] + pin[s, m]
            if s == 0:
                relay_out(m).start()
        if s > 0:
            reduce_out(s, 1 - k).start()

    def relay_sum(s):
        relay_in(s - 1).wait_recv()
        part[s, k, k] = part[s, k, k] + relay[s - 1]
        reduce_out(s, k).start()

    def back(m, j, slot):
        return rcopy(
            img.at[m, j], held[m].at[pl.ds(slot * 4, 4)], s4.at[m, j], r4.at[m, slot], (row, j)
        )

    def home(m, j, slot):
        return rcopy(
            ob.at[m, pl.ds(j * SLOTS, SLOTS)], fin.at[m, slot], s5.at[m, j], r5.at[m, slot],
            (row, j),
        )

    def finish(m):
        exchange(last, m).wait_recv()
        reduce_in(0, m).wait_recv()
        reduce_in(1, m).wait_recv()
        v = part[last, k, m] + pin[last, m] + rin[0, m] + rin[1, m]
        v = v.reshape(4, COLS, 1, 8, LANES)
        for b in range(4):
            img[m, :, b : b + 1] = v[b]

        @pl.loop(1, COLS)
        def _(d):
            back(m, (col + d) % COLS, col).start()

        held[m][pl.ds(col * 4, 4)] = img[m, col]

    def send_home(m):
        @pl.loop(1, COLS)
        def _(d):
            j = (col + COLS - d) % COLS
            back(m, j, j).wait_recv()

        @pl.loop(0, COLS * SLOTS, unroll=32)
        def _(i):
            ob[m, i] = held[m][jnp.maximum(tblk[i], 0)]

        @pl.loop(1, COLS)
        def _(d):
            home(m, (col + d) % COLS, col).start()

        fin[m, col] = ob[m, pl.ds(col * SLOTS, SLOTS)]

    rows_arrived(3)
    start(3, 0)
    rows_arrived(0)
    start(0, 0)
    rows_arrived(1)
    start(1, 0)
    arrived(3, 0)
    start(3, 1)
    rows_arrived(2)
    start(2, 0)
    for s in range(3):
        arrived(s, 0)
        start(s, 1)
    arrived(0, 1)
    start(0, 2, 3)
    arrived(1, 1)
    start(1, 2)
    arrived(0, 2)
    start(0, 4)
    start(1, 3)
    arrived(2, 1)
    start(2, 2)
    arrived(0, 3)
    near_part(0)
    arrived(1, 2)
    start(1, 4)
    start(2, 3)
    arrived(0, 4)
    far_part(0)
    row_sums(0)
    arrived(1, 3)
    near_part(1)
    arrived(2, 2)
    start(2, 4)
    arrived(3, 1)
    start(3, 2, 3)
    arrived(1, 4)
    far_part(1)
    row_sums(1)
    arrived(2, 3)
    relay_sum(1)
    near_part(2)
    arrived(2, 4)
    far_part(2)
    row_sums(2)
    relay_sum(2)
    arrived(3, 2)
    start(3, 4)
    arrived(3, 3)
    near_part(3)
    arrived(3, 4)
    far_part(3)
    finish(0)
    finish(1)
    send_home(0)
    send_home(1)

    def homed(m):
        @pl.loop(1, COLS)
        def _(d):
            j = (col + COLS - d) % COLS
            home(m, j, j).wait_recv()

    def returned(s, m):
        v = fin[m, :, s].reshape(LANES, LANES)
        hot = onehot[s, :, m * LANES : (m + 1) * LANES]
        return sum3(jnp.dot(hot, split3(v), preferred_element_type=F32))

    homed(0)
    for s in range(SLOTS):
        diag = jnp.sum(
            jnp.where(row_iota == col_iota, energy[s : s + 1, :], 0.0), axis=1, keepdims=True
        )
        out[s] = diag * amp[s] + returned(s, 0)
    homed(1)
    for s in range(SLOTS):
        live = (s < counts[col]).astype(F32)
        out[s] = (out[s] + returned(s, 1)) * live

    @pl.loop(1, COLS)
    def _(d):
        j = (col + d) % COLS
        spread(j, col).wait_send()
        for m in range(2):
            back(m, j, col).wait_send()
            home(m, j, col).wait_send()

    for c in rows_sent:
        c.wait_send()

    for s in range(STEPS):
        for kind in range(5):
            for c in gather(s, kind, True):
                c.wait_send()
        for m in range(2):
            exchange(s, m).wait_send()
    for m in range(2):
        relay_out(m).wait_send()
        for s in (1, 2):
            reduce_out(s, m).wait_send()


def local(
    amplitudes, interaction, tile_counts, tile_block, recouple_sign, orbit_perm, particle_energy
):
    w = interaction.reshape(8, COLS, PIECE, 1024)
    smem = pl.BlockSpec(memory_space=pltpu.SMEM)
    vmem = pl.BlockSpec(memory_space=pltpu.VMEM)
    dma = pltpu.SemaphoreType.DMA
    return pl.pallas_call(
        kernel,
        out_shape=jax.ShapeDtypeStruct(amplitudes.shape, F32),
        in_specs=[smem] * 3 + [vmem] * 3 + [pl.BlockSpec(memory_space=pl.ANY)],
        out_specs=vmem,
        scratch_shapes=[
            pltpu.VMEM((8, LANES), jnp.int32),
            pltpu.SMEM((8, LANES), jnp.int32),
            pltpu.VMEM((SLOTS, TILE, TILE), BF16),
            pltpu.VMEM((COLS, SLOTS, PIECE, LANES), F32),
            pltpu.VMEM((COLS * SLOTS, PIECE, LANES), F32),
            pltpu.VMEM((64, PIECE, LANES), F32),
            pltpu.VMEM((STEPS, 4, 4, 2, 4, PIECE, LANES), F32),
            pltpu.VMEM((STEPS, 4, 4, 2, 4, PIECE, LANES), F32),
            pltpu.VMEM((4, 4, 8, PIECE, 1024), F32),
            pltpu.VMEM((1024, 2048), BF16),
            pltpu.VMEM((1024, 2048), BF16),
            pltpu.VMEM((2048, TILE), BF16),
            pltpu.VMEM((2048, TILE), BF16),
            pltpu.VMEM((STEPS, 2, 2, HALF, LANES), F32),
            pltpu.VMEM((STEPS, 2, HALF, LANES), F32),
            pltpu.VMEM((2, HALF, LANES), F32),
            pltpu.VMEM((2, 2, HALF, LANES), F32),
            pltpu.VMEM((2, COLS, 4, 8, LANES), F32),
            pltpu.VMEM((64, 8, LANES), F32),
            pltpu.VMEM((64, 8, LANES), F32),
            pltpu.VMEM((2, COLS * SLOTS, 8, LANES), F32),
            pltpu.VMEM((2, COLS, SLOTS, 8, LANES), F32),
            dma,
            dma((COLS,)),
            dma((COLS,)), dma((COLS,)),
            dma((ROWS, 2)), dma((ROWS, 2)),
            dma((STEPS, 5, 4)), dma((STEPS, 5, 4)),
            dma((STEPS, 2)), dma((STEPS, 2)),
            dma((2,)), dma((2,)),
            dma((2, 2)), dma((2, 2)),
            dma((2, COLS)), dma((2, COLS)),
            dma((2, COLS)), dma((2, COLS)),
        ],
        compiler_params=pltpu.CompilerParams(
            collective_id=0, has_side_effects=True, vmem_limit_bytes=60 * 1024 * 1024
        ),
        name="sigma_step",
    )(tile_counts, tile_block, recouple_sign, amplitudes, orbit_perm, particle_energy, w)


def solution(mesh):
    placed = (P("col", None, "row"), P("row", "col"), P(), P(), P(), P(), P("col", None))
    return jax.shard_map(
        local, mesh=mesh, in_specs=placed, out_specs=P("col", None, "row"), check_vma=False
    )
```

```python
import functools

import jax
import jax.numpy as jnp
from jax import lax
from jax.experimental import pallas as pl
from jax.experimental.pallas import tpu as pltpu
from jax.sharding import PartitionSpec as P

MESH = pl.DeviceIdType.MESH
F32, BF16 = jnp.float32, jnp.bfloat16
ROWS, COLS = 8, 16
SLOTS, TILE, LANES = 6, 256, 128
PIECE = TILE // COLS
STEPS = 4
HALF = 512


def split3(v):
    a = v.astype(BF16)
    rest = v - a.astype(F32)
    b = rest.astype(BF16)
    d = (rest - b.astype(F32)).astype(BF16)
    return jnp.concatenate([a, b, d], axis=1)


def sum3(v):
    return v[:, :LANES] + v[:, LANES : 2 * LANES] + v[:, 2 * LANES :]


def kernel(
    counts, tblk, signs, amp, perm, energy, w_hbm, out, slot_row, slot_of,
    onehot, send1, recv1, sel, xa, xc, wst, whi, wlo, xhi, xlo, part, pin, relay, rin,
    img, gb0, gb1, ob, fin,
    isem, wsem, s1, r1, s2, r2, sx, rx, sp, rp, sy, ry, sr, rr, s4, r4, s5, r5,
):
    row, col = lax.axis_index("row"), lax.axis_index("col")
    y, k = row // 2, row % 2
    z, x = col // 4, col % 4
    zp, zm, z2 = (z + 1) % 4, (z + 3) % 4, (z + 2) % 4
    xp, xm, x2 = (x + 1) % 4, (x + 3) % 4, (x + 2) % 4
    yp, ym, y2 = (y + 1) % 4, (y + 3) % 4, (y + 2) % 4
    partner = row + 1 - 2 * k
    last = STEPS - 1
    held = (gb0, gb1)

    def rcopy(src, dst, ssem, rsem, to):
        return pltpu.make_async_remote_copy(
            src_ref=src, dst_ref=dst, send_sem=ssem, recv_sem=rsem,
            device_id=to, device_id_type=MESH,
        )

    barrier = pltpu.get_barrier_semaphore()

    @pl.loop(1, COLS)
    def _(d):
        pl.semaphore_signal(barrier, inc=1, device_id=(row, (col + d) % COLS), device_id_type=MESH)

    @pl.loop(1, ROWS)
    def _(d):
        pl.semaphore_signal(barrier, inc=1, device_id=((row + d) % ROWS, col), device_id_type=MESH)

    def wcopy(j):
        return pltpu.make_async_copy(w_hbm.at[:, j], wst.at[j // 4, j % 4], wsem.at[j])

    @pl.loop(0, COLS)
    def _(j):
        wcopy(j).start()

    lane = lax.broadcasted_iota(jnp.int32, (8, LANES), 1)
    found = jnp.zeros((8, LANES), jnp.int32)
    for i in range(COLS * SLOTS):
        found = jnp.where(lane == tblk[i], i, found)
    slot_row[...] = found
    to_scalars = pltpu.make_async_copy(slot_row, slot_of, isem)
    to_scalars.start()

    row_iota = lax.broadcasted_iota(jnp.int32, (TILE, TILE), 0)
    col_iota = lax.broadcasted_iota(jnp.int32, (TILE, TILE), 1)

    @pl.loop(0, SLOTS)
    def _(s):
        order = perm[pl.ds(col * SLOTS + s, 1), :]
        phase = (1 - 2 * signs[col * SLOTS + s]).astype(F32)
        hot = jnp.where(row_iota == order, phase, 0.0)
        onehot[s] = hot.astype(BF16)
        moved = sum3(
            jnp.dot(hot.T.astype(BF16), split3(amp[s]), preferred_element_type=F32)
        )
        send1[:, pl.ds(s, 1)] = moved.reshape(COLS, 1, PIECE, LANES)

    pl.semaphore_wait(barrier, COLS - 1 + ROWS - 1)

    def spread(j, slot):
        return rcopy(
            send1.at[j], recv1.at[pl.ds(slot * SLOTS, SLOTS)], s1.at[j], r1.at[slot], (row, j)
        )

    @pl.loop(1, COLS)
    def _(d):
        spread((col + d) % COLS, col).start()

    recv1[pl.ds(col * SLOTS, SLOTS)] = send1[col]

    @pl.loop(0, COLS)
    def _(j):
        wcopy(j).wait()

    def shift_of(n):
        return n + n // 2 - 2 * (n // 3)

    def place_a(n):
        return pl.ds(pl.multiple_of((n + 3 * (n // 3)) * TILE, TILE), TILE)

    def place_c(n):
        return pl.ds(pl.multiple_of((n + 3 + n // 3) * TILE, TILE), TILE)

    def weights(v, b, at):
        v = v.reshape(TILE, TILE).T
        hi = v.astype(BF16)
        lo = (v - hi.astype(F32)).astype(BF16)
        for m in range(2):
            rows_at = slice(m * HALF + b * LANES, m * HALF + (b + 1) * LANES)
            whi[rows_at, at] = hi[m * LANES : (m + 1) * LANES]
            wlo[rows_at, at] = lo[m * LANES : (m + 1) * LANES]

    @pl.loop(0, 4)
    def _(n):
        zn, xn = (z + shift_of(n)) % 4, (x + shift_of(n)) % 4
        for b in range(4):
            cut = slice(b * TILE, (b + 1) * TILE)
            weights(wst[zn, :, 0:4, :, cut], b, place_a(n))
            weights(wst[:, xn, 4:8, :, cut], b, place_c(n))

    @pl.loop(1, COLS)
    def _(d):
        j = (col + COLS - d) % COLS
        spread(j, j).wait_recv()

    to_scalars.wait()

    def select(first, count):
        @pl.loop(0, count, unroll=16)
        def _(n):
            g = (first + n) % 64
            sel[g] = recv1[slot_of[0, g]]

    select(16 * y2, 16)

    def rows_copies(r, source, slot):
        return [
            rcopy(
                sel.at[pl.ds(r * 8, 4)], xa.at[slot[0], z, x, slot[1]],
                s2.at[r, 0], r2.at[source, 0], (r, col),
            ),
            rcopy(
                sel.at[pl.ds(r * 8 + 4, 4)], xc.at[slot[0], x, z, slot[1]],
                s2.at[r, 1], r2.at[source, 1], (r, col),
            ),
        ]

    rows_sent = [
        c
        for r, slot in (
            (2 * y2, (0, k)), (2 * y2 + 1, (0, k)),
            (2 * ym, (1 + k, 0)), (2 * yp, (1 + k, 1)),
            (2 * ym + 1, (1 + k, 0)), (2 * yp + 1, (1 + k, 1)),
            (partner, (3, k)),
        )
        for c in rows_copies(r, row, slot)
    ]
    for c in rows_sent[:4]:
        c.start()
    select(16 * y2 + 16, 48)
    for c in rows_sent[4:]:
        c.start()

    xa[3, z, x, k] = sel[pl.ds(row * 8, 4)]
    xc[3, x, z, k] = sel[pl.ds(row * 8 + 4, 4)]

    def rows_arrived(s):
        for r, slot in (
            ((2 * y2, (0, 0)), (2 * y2 + 1, (0, 1))),
            ((2 * yp, (1, 0)), (2 * ym, (1, 1))),
            ((2 * yp + 1, (2, 0)), (2 * ym + 1, (2, 1))),
            ((partner, (3, 1 - k)),),
        )[s]:
            for c in rows_copies(r, r, slot):
                c.wait_recv()

    to_x = ((row, z * 4 + xp), (row, z * 4 + xm))
    to_z = ((row, zp * 4 + x), (row, zm * 4 + x))

    def gather(s, kind, sends):
        lo, up = slice(0, 2), slice(2, 4)
        if kind == 0:
            here, there = ((z, x), (z, x), (x, z), (x, z)), ((z, xm), (z, xp), (x, zm), (x, zp))
        elif kind == 1:
            here = ((z, xm, 0), (z, xp, 1), (x, zm, 0), (x, zp, 1))
            there = ((z, x2, 0), (z, x2, 1), (x, z2, 0), (x, z2, 1))
        elif kind == 2:
            here = ((z, lo), (z, up), (x, lo), (x, up))
            there = ((zm, lo), (zp, up), (xm, lo), (xp, up))
        elif kind == 3:
            here = ((z, up), (z, lo), (x, up), (x, lo))
            there = ((zm, up), (zp, lo), (xm, up), (xp, lo))
        else:
            here = ((zm, lo), (zp, up), (xm, lo), (xp, up))
            there = ((z2, lo), (z2, up), (x2, lo), (x2, up))
        to = to_x + to_z if kind < 2 else to_z + to_x
        copies = []
        for n, at in enumerate(here if sends else there):
            ref = (xa, xa, xc, xc)[n].at[(s,) + at]
            copies.append(rcopy(ref, ref, sx.at[s, kind, n], rx.at[s, kind, n], to[n]))
        return copies

    def start(s, *kinds):
        for kind in kinds:
            for c in gather(s, kind, True):
                c.start()

    def arrived(s, *kinds):
        for kind in kinds:
            for c in gather(s, kind, False):
                c.wait_recv()

    def exchange(s, m):
        return rcopy(
            part.at[s, 1 - k, m], pin.at[s, m], sp.at[s, m], rp.at[s, m], (partner, col)
        )

    def relay_copy(m, slot, to):
        return rcopy(part.at[0, k, m], relay.at[slot], sy.at[m], ry.at[slot], to)

    def relay_out(m):
        return relay_copy(m, k, (2 * yp, col) if m == 0 else (2 * ym + 1, col))

    def relay_in(slot):
        return relay_copy(0, slot, (partner, col))

    def reduce_out(s, m):
        q = yp + k * (ym - yp)
        return rcopy(
            part.at[s, k, m], rin.at[k, m], sr.at[s - 1, m], rr.at[k, m], (2 * q + s - 1, col)
        )

    def reduce_in(n, m):
        return rcopy(part.at[1, k, m], rin.at[n, m], sr.at[0, m], rr.at[n, m], (partner, col))

    def dots(s, m, first):
        rows_at = slice(m * HALF, (m + 1) * HALF)
        cut = slice(0, 6 * TILE) if first else slice(6 * TILE, 8 * TILE)
        hi = whi[rows_at, cut]
        both = jnp.concatenate([hi, wlo[rows_at, cut]], axis=0)
        both = jnp.dot(both, xhi[cut], preferred_element_type=F32)
        acc = jnp.dot(hi, xlo[cut], preferred_element_type=F32)
        acc += both[HALF:] + both[:HALF]
        for n in range(2):
            v = acc[:, n * LANES : (n + 1) * LANES]
            part[s, n, m] = v if first else part[s, n, m] + v

    def convert(v0, v1, at):
        v = jnp.concatenate([v0.reshape(TILE, LANES), v1.reshape(TILE, LANES)], axis=1)
        hi = v.astype(BF16)
        xhi[at, :] = hi
        xlo[at, :] = (v - hi.astype(F32)).astype(BF16)

    def convert_lines(s, low, high):
        @pl.loop(low, high)
        def _(n):
            zn, xn = (z + shift_of(n)) % 4, (x + shift_of(n)) % 4
            convert(xa[s, zn, :, 0], xa[s, zn, :, 1], place_a(n))
            convert(xc[s, xn, :, 0], xc[s, xn, :, 1], place_c(n))

    def near_part(s):
        convert_lines(s, 0, 3)
        dots(s, 0, True)
        dots(s, 1, True)

    def far_part(s):
        convert_lines(s, 3, 4)
        for m in range(2):
            dots(s, m, False)
            exchange(s, m).start()

    def row_sums(s):
        for m in range(2):
            exchange(s, m).wait_recv()
            part[s, k, m] = part[s, k, m] + pin[s, m]
            if s == 0:
                relay_out(m).start()
        if s > 0:
            reduce_out(s, 1 - k).start()

    def relay_sum(s):
        relay_in(s - 1).wait_recv()
        part[s, k, k] = part[s, k, k] + relay[s - 1]
        reduce_out(s, k).start()

    def back(m, j, slot):
        return rcopy(
            img.at[m, j], held[m].at[pl.ds(slot * 4, 4)], s4.at[m, j], r4.at[m, slot], (row, j)
        )

    def home(m, j, slot):
        return rcopy(
            ob.at[m, pl.ds(j * SLOTS, SLOTS)], fin.at[m, slot], s5.at[m, j], r5.at[m, slot],
            (row, j),
        )

    def finish(m):
        exchange(last, m).wait_recv()
        reduce_in(0, m).wait_recv()
        reduce_in(1, m).wait_recv()
        v = part[last, k, m] + pin[last, m] + rin[0, m] + rin[1, m]
        v = v.reshape(4, COLS, 1, 8, LANES)
        for b in range(4):
            img[m, :, b : b + 1] = v[b]

        @pl.loop(1, COLS)
        def _(d):
            back(m, (col + d) % COLS, col).start()

        held[m][pl.ds(col * 4, 4)] = img[m, col]

    def send_home(m):
        @pl.loop(1, COLS)
        def _(d):
            j = (col + COLS - d) % COLS
            back(m, j, j).wait_recv()

        @pl.loop(0, COLS * SLOTS, unroll=32)
        def _(i):
            ob[m, i] = held[m][jnp.maximum(tblk[i], 0)]

        @pl.loop(1, COLS)
        def _(d):
            home(m, (col + d) % COLS, col).start()

        fin[m, col] = ob[m, pl.ds(col * SLOTS, SLOTS)]

    rows_arrived(3)
    start(3, 0)
    rows_arrived(0)
    start(0, 0)
    rows_arrived(1)
    start(1, 0)
    arrived(3, 0)
    start(3, 1)
    rows_arrived(2)
    start(2, 0)
    for s in range(3):
        arrived(s, 0)
        start(s, 1)
    arrived(0, 1)
    start(0, 2, 3)
    arrived(1, 1)
    start(1, 2)
    arrived(0, 2)
    start(0, 4)
    start(1, 3)
    arrived(2, 1)
    start(2, 2)
    arrived(0, 3)
    near_part(0)
    arrived(1, 2)
    start(1, 4)
    start(2, 3)
    arrived(0, 4)
    far_part(0)
    row_sums(0)
    arrived(1, 3)
    near_part(1)
    arrived(2, 2)
    start(2, 4)
    arrived(3, 1)
    start(3, 2, 3)
    arrived(1, 4)
    far_part(1)
    row_sums(1)
    arrived(2, 3)
    relay_sum(1)
    near_part(2)
    arrived(2, 4)
    far_part(2)
    row_sums(2)
    relay_sum(2)
    arrived(3, 2)
    start(3, 4)
    arrived(3, 3)
    near_part(3)
    arrived(3, 4)
    far_part(3)
    finish(0)
    finish(1)
    send_home(0)
    send_home(1)

    def homed(m):
        @pl.loop(1, COLS)
        def _(d):
            j = (col + COLS - d) % COLS
            home(m, j, j).wait_recv()

    def returned(s, m):
        v = fin[m, :, s].reshape(LANES, LANES)
        hot = onehot[s, :, m * LANES : (m + 1) * LANES]
        return sum3(jnp.dot(hot, split3(v), preferred_element_type=F32))

    homed(0)
    for s in range(SLOTS):
        diag = jnp.sum(
            jnp.where(row_iota == col_iota, energy[s : s + 1, :], 0.0), axis=1, keepdims=True
        )
        out[s] = diag * amp[s] + returned(s, 0)
    homed(1)
    for s in range(SLOTS):
        live = (s < counts[col]).astype(F32)
        out[s] = (out[s] + returned(s, 1)) * live

    @pl.loop(1, COLS)
    def _(d):
        j = (col + d) % COLS
        spread(j, col).wait_send()
        for m in range(2):
            back(m, j, col).wait_send()
            home(m, j, col).wait_send()

    for c in rows_sent:
        c.wait_send()

    for s in range(STEPS):
        for kind in range(5):
            for c in gather(s, kind, True):
                c.wait_send()
        for m in range(2):
            exchange(s, m).wait_send()
    for m in range(2):
        relay_out(m).wait_send()
        for s in (1, 2):
            reduce_out(s, m).wait_send()


def local(
    amplitudes, interaction, tile_counts, tile_block, recouple_sign, orbit_perm, particle_energy
):
    w = interaction.reshape(8, COLS, PIECE, 1024)
    smem = pl.BlockSpec(memory_space=pltpu.SMEM)
    vmem = pl.BlockSpec(memory_space=pltpu.VMEM)
    dma = pltpu.SemaphoreType.DMA
    return pl.pallas_call(
        kernel,
        out_shape=jax.ShapeDtypeStruct(amplitudes.shape, F32),
        in_specs=[smem] * 3 + [vmem] * 3 + [pl.BlockSpec(memory_space=pl.ANY)],
        out_specs=vmem,
        scratch_shapes=[
            pltpu.VMEM((8, LANES), jnp.int32),
            pltpu.SMEM((8, LANES), jnp.int32),
            pltpu.VMEM((SLOTS, TILE, TILE), BF16),
            pltpu.VMEM((COLS, SLOTS, PIECE, LANES), F32),
            pltpu.VMEM((COLS * SLOTS, PIECE, LANES), F32),
            pltpu.VMEM((64, PIECE, LANES), F32),
            pltpu.VMEM((STEPS, 4, 4, 2, 4, PIECE, LANES), F32),
            pltpu.VMEM((STEPS, 4, 4, 2, 4, PIECE, LANES), F32),
            pltpu.VMEM((4, 4, 8, PIECE, 1024), F32),
            pltpu.VMEM((1024, 2048), BF16),
            pltpu.VMEM((1024, 2048), BF16),
            pltpu.VMEM((2048, TILE), BF16),
            pltpu.VMEM((2048, TILE), BF16),
            pltpu.VMEM((STEPS, 2, 2, HALF, LANES), F32),
            pltpu.VMEM((STEPS, 2, HALF, LANES), F32),
            pltpu.VMEM((2, HALF, LANES), F32),
            pltpu.VMEM((2, 2, HALF, LANES), F32),
            pltpu.VMEM((2, COLS, 4, 8, LANES), F32),
            pltpu.VMEM((64, 8, LANES), F32),
            pltpu.VMEM((64, 8, LANES), F32),
            pltpu.VMEM((2, COLS * SLOTS, 8, LANES), F32),
            pltpu.VMEM((2, COLS, SLOTS, 8, LANES), F32),
            dma,
            dma((COLS,)),
            dma((COLS,)), dma((COLS,)),
            dma((ROWS, 2)), dma((ROWS, 2)),
            dma((STEPS, 5, 4)), dma((STEPS, 5, 4)),
            dma((STEPS, 2)), dma((STEPS, 2)),
            dma((2,)), dma((2,)),
            dma((2, 2)), dma((2, 2)),
            dma((2, COLS)), dma((2, COLS)),
            dma((2, COLS)), dma((2, COLS)),
        ],
        compiler_params=pltpu.CompilerParams(
            collective_id=0, has_side_effects=True, vmem_limit_bytes=60 * 1024 * 1024
        ),
        name="sigma_step",
    )(tile_counts, tile_block, recouple_sign, amplitudes, orbit_perm, particle_energy, w)


def solution(mesh):
    placed = (P("col", None, "row"), P("row", "col"), P(), P(), P(), P(), P("col", None))
    return jax.shard_map(
        local, mesh=mesh, in_specs=placed, out_specs=P("col", None, "row"), check_vma=False
    )
```
